32 devices in a mesh: dp: 2 (over x), expert: 16 (over z, y, core).
Axes of the slice: x: 2, y: 2, z: 4, core: 2. Of those that a mesh axis runs over, the one named last changes fastest.
Arguments:
- tokens: bfloat16 [2048, 2560], P('expert', 'dp'), may hold values from -6 to 6
- cotangent: bfloat16 [2048, 2560], P('expert', 'dp'), may hold values from -6 to 6
- expert_ids: int32 [2048, 6], P('expert'), may hold values from 0 to 15, all different within a row; in each aligned block of 128 rows (0 to 127, 128 to 255, ...) at most 64 rows name the same one
- gate_weights: float32 [2048, 6], P('expert'), may hold values from 0.1 to 0.6
- w_in: bfloat16 [16, 2560, 768], P('expert', 'dp'), may hold values from -0.125 to 0.125
- w_out: bfloat16 [16, 768, 2560], P('expert', None, 'dp'), may hold values from -0.21875 to 0.21875
Outputs:
- mixed_out: bfloat16 [2048, 2560], P('expert', 'dp')
- token_grad: bfloat16 [2048, 2560], P('expert', 'dp')
- w_in_grad: bfloat16 [16, 2560, 768], P('expert', 'dp')
- w_out_grad: bfloat16 [16, 768, 2560], P('expert', None, 'dp')
The draws below stay inside these ranges and needn't reach their ends.
Inputs may be any that keep to these rules, and one draw needn't show every extreme that they name: `expert_ids`: each row names 6 different experts. Within the rows of one device (aligned blocks of 128 rows) no expert is named more than 64 times, a bound that some block reaches.
All inputs are finite; a program needn't handle non-finite values.
Results may differ from the reference program's by a relative error of at most 0.017.
Values may be sent and summed in bfloat16 or wider, within the bound.
A program may use at most 64 MiB of HBM per device.

```python
import math
import jax
import jax.numpy as jnp
import numpy as np
from jax import lax

D = 2560
F = 768
TOP = 6
TOK_DEV = 128
EXPERTS = 16
TOKENS = 2048
CAP = 64
N_DP = 2
N_EXPERT = 16


def shard_levels(own_key, extent, split, smallest, top_value):
    def one(axis_at, blocks):
        draws = jax.random.uniform(jax.random.fold_in(jax.random.fold_in(own_key, 6), axis_at), (blocks,), jnp.float32, smallest / len(split), top_value / len(split))
        return jnp.repeat(jnp.exp(draws), extent[axis_at] // blocks).reshape((-1,) + (1,) * (len(extent) - axis_at - 1))

    loudness = one(*split[0])
    for cut in split[1:]:
        loudness = loudness * one(*cut)
    return loudness


def deal_out(rng, own, number, rows, amount, top, most, lean):
    ranking = jax.random.permutation(rng, amount)
    packed, ordinary = load_shares(amount, rows * top, most, lean, True), load_shares(amount, rows * top, most, lean, False)
    places = jnp.arange(amount)

    def named(lengths, turn):
        used = int((lengths > 0).sum())
        fixed = max(1, used // 4)
        shifted = fixed + (places - fixed + turn * (used - fixed)) % max(1, amount - fixed)
        return jnp.zeros((amount,), jnp.int32).at[ranking[jnp.where(places < fixed, places, shifted)]].set(jnp.asarray(lengths, jnp.int32))

    lengths = jnp.where(number % 4 == 0, named(packed, number // 4), named(ordinary, number - number // 4 - 1))
    mixed = jax.random.permutation(jax.random.fold_in(own, 3), amount)
    source_of, taker = mixed[0:amount // 2 * 2:2], mixed[1:amount // 2 * 2:2]
    room = jnp.minimum(lengths[source_of] - 1, most - lengths[taker]) // 2
    room = jnp.where((source_of == ranking[0]) | (taker == ranking[0]) | (lengths[taker] == 0), 0, jnp.maximum(room, 0))
    shifted = jax.random.randint(jax.random.fold_in(own, 4), (amount // 2,), 0, 1 << 20) % (room + 1)
    lengths = lengths.at[source_of].add(-shifted).at[taker].add(shifted)
    members = jnp.searchsorted(jnp.cumsum(lengths), jnp.arange(rows * top), side="right").astype(jnp.int32)
    table = members.reshape(top, rows).T
    table = table[jax.random.permutation(jax.random.fold_in(own, 1), rows)]
    turn = jax.random.randint(jax.random.fold_in(own, 2), (rows, 1), 0, top)
    return jnp.take_along_axis(table, (jnp.arange(top)[None, :] + turn) % top, axis=1)


def load_shares(count, total, most, lean, full):
    loads = [(1 << 20) // math.isqrt(rank ** lean) + 1 for rank in range(1, count + 1)]
    largest = most if full else min(most, max(-(-total // count), total * loads[0] // sum(loads)))
    least = 1 if total - largest >= count - 1 else 0
    counts, surplus = [largest] + [least] * (count - 1), total - largest - least * (count - 1)
    while surplus > 0:
        movable = [i for i in range(1, count) if counts[i] < largest] or [i for i in range(1, count) if counts[i] < most]
        whole, remaining = sum([loads[i] for i in movable]), surplus
        for i in movable:
            addition = min(most - counts[i], max(1, remaining * loads[i] // whole), surplus)
            counts[i] = counts[i] + addition
            surplus = surplus - addition
    return np.array(counts)


def noise(rng, dims, deviation, limit, shards=(), held_as=jnp.bfloat16):
    level = shard_levels(rng, dims, shards, -0.22, 0.18) if shards else 1.0
    drawn = jax.random.normal(rng, dims, jnp.float32) * deviation * level
    return jnp.minimum(jnp.maximum(drawn, -limit), limit).astype(held_as)


def setup_inputs(seed: int = 0) -> dict:
    streams_of = jax.random.split(jax.random.key(seed), 7)
    tokens = noise(streams_of[0], (TOKENS, D), 1.0, 6.0, ((0, 16), (1, 2)))
    cotangent = noise(streams_of[1], (TOKENS, D), 1.0, 6.0, ((0, 16), (1, 2)))
    expert_ids_keys = jax.random.split(jax.random.fold_in(streams_of[2], 1), TOKENS // TOK_DEV)
    expert_ids_turns = jax.random.permutation(jax.random.fold_in(streams_of[2], 3), TOKENS // TOK_DEV)
    expert_ids = jax.vmap(lambda own, number: deal_out(jax.random.fold_in(streams_of[2], 2), own, number, TOK_DEV, EXPERTS, TOP, CAP, 2))(expert_ids_keys, expert_ids_turns).reshape((TOKENS, TOP))
    gate_weights = jnp.clip(0.1 + 0.5 * jax.random.uniform(streams_of[3], (TOKENS, TOP), jnp.float32) ** shard_levels(streams_of[3], (TOKENS, TOP), ((0, 16),), -0.2, 0.2), 0.1, 0.6)
    w_in = noise(streams_of[4], (EXPERTS, D, F), D ** -0.5, 0.125, ((0, 16), (1, 2)))
    w_out = noise(streams_of[5], (EXPERTS, F, D), F ** -0.5, 0.21875, ((0, 16), (2, 2)))
    return {"tokens": tokens, "cotangent": cotangent, "expert_ids": expert_ids, "gate_weights": gate_weights, "w_in": w_in, "w_out": w_out}


def silu_slope(hidden_value):
    logistic = jax.nn.sigmoid(hidden_value)
    return logistic * (1.0 + hidden_value * (1.0 - logistic))


def rounded(hidden_value):
    return lax.optimization_barrier(hidden_value.astype(jnp.bfloat16)).astype(jnp.float32)


def reference(tokens, cotangent, expert_ids, gate_weights, w_in, w_out):
    assign = TOKENS * TOP
    slots_each = N_EXPERT * CAP
    quarter = D // N_DP
    flat_ids = expert_ids.reshape(-1).astype(jnp.int32)
    onehot = (flat_ids[:, None] == jnp.arange(EXPERTS, dtype=jnp.int32)[None, :]).astype(jnp.int32)
    earlier = jnp.sum((jnp.cumsum(onehot, axis=0) - onehot) * onehot, axis=1).astype(jnp.int32)
    slot_table = jnp.full((EXPERTS * slots_each,), assign, jnp.int32)
    slot_table = slot_table.at[flat_ids * slots_each + earlier].set(jnp.arange(assign, dtype=jnp.int32))
    slot_table = slot_table.reshape(EXPERTS, slots_each)
    zero_row = jnp.zeros((1, D), tokens.dtype)
    padded_x = jnp.concatenate([tokens, zero_row], 0)
    padded_dy = jnp.concatenate([cotangent, zero_row], 0)
    padded_gate = jnp.concatenate([gate_weights.reshape(-1), jnp.zeros((1,), jnp.float32)], 0)

    def per_expert(totals, inputs):
        mixed_acc, grad_acc = totals
        slot_source, weight_in, weight_out = inputs
        token_row = (slot_source // TOP).astype(jnp.int32)
        gate_value = padded_gate[slot_source]
        rows_x = padded_x[token_row]
        rows_dy = (gate_value[:, None] * padded_dy[token_row].astype(jnp.float32)).astype(jnp.bfloat16)
        preact = jnp.zeros((slots_each, F), jnp.float32)
        slope_total = jnp.zeros((slots_each, F), jnp.float32)
        for quarter_index in range(N_DP):
            start_col = quarter_index * quarter
            stop_col = start_col + quarter
            preact = preact + rounded(jnp.dot(rows_x[:, start_col:stop_col], weight_in[start_col:stop_col], preferred_element_type=jnp.float32))
            slope_total = slope_total + rounded(jnp.dot(rows_dy[:, start_col:stop_col], weight_out[:, start_col:stop_col].T, preferred_element_type=jnp.float32))
        activation = jax.nn.silu(preact).astype(jnp.bfloat16)
        out_rows = rounded(jnp.dot(activation, weight_out, preferred_element_type=jnp.float32))
        mixed_acc = mixed_acc.at[token_row].add(gate_value[:, None] * out_rows)
        delta_hidden = (slope_total * silu_slope(preact)).astype(jnp.bfloat16)
        out_grad = jnp.dot(activation.T, rows_dy, preferred_element_type=jnp.float32).astype(jnp.bfloat16)
        in_grad = jnp.dot(rows_x.T, delta_hidden, preferred_element_type=jnp.float32).astype(jnp.bfloat16)
        back_rows = rounded(jnp.dot(delta_hidden, weight_in.T, preferred_element_type=jnp.float32))
        grad_acc = grad_acc.at[token_row].add(back_rows)
        return (mixed_acc, grad_acc), (in_grad, out_grad)

    start_totals = (jnp.zeros((TOKENS + 1, D), jnp.float32), jnp.zeros((TOKENS + 1, D), jnp.float32))
    (mixed_acc, grad_acc), (in_grads, out_grads) = lax.scan(per_expert, start_totals, (slot_table, w_in, w_out))
    return (mixed_acc[:TOKENS].astype(jnp.bfloat16), grad_acc[:TOKENS].astype(jnp.bfloat16), in_grads, out_grads)
```

```python
import functools

import jax
import jax.numpy as jnp
from jax import lax
from jax.experimental import pallas as pl
from jax.experimental.pallas import tpu as pltpu
from jax.sharding import PartitionSpec as P


def silu_slope(hidden_value):
    logistic = jax.nn.sigmoid(hidden_value)
    return logistic * (1.0 + hidden_value * (1.0 - logistic))


def expert_hidden(rows_x, weight_in):
    partial_sum = jnp.dot(rows_x, weight_in, preferred_element_type=jnp.float32)
    share_sum = lax.psum_scatter(
        partial_sum.astype(jnp.bfloat16), "dp", scatter_dimension=1, tiled=True
    ).astype(jnp.float32)
    share_act = jax.nn.silu(share_sum).astype(jnp.bfloat16)
    return (share_sum, lax.all_gather(share_act, "dp", axis=1, tiled=True))


def expert_slope(rows_dy, weight_out, preact):
    partial_sum = lax.dot_general(
        rows_dy, weight_out, (((1,), (1,)), ((), ())), preferred_element_type=jnp.float32
    )
    share_sum = lax.psum_scatter(
        partial_sum.astype(jnp.bfloat16), "dp", scatter_dimension=1, tiled=True
    ).astype(jnp.float32)
    share_delta = (share_sum * silu_slope(preact)).astype(jnp.bfloat16)
    return lax.all_gather(share_delta, "dp", axis=1, tiled=True)


def local_slots(tokens, cotangent, expert_ids, gate_weights, w_in, w_out):
    experts = lax.axis_size("expert")
    tok_rows, quarter = tokens.shape
    choose_count = expert_ids.shape[1]
    capacity = max(2, 4 * tok_rows * choose_count // (3 * experts))
    assign = tok_rows * choose_count
    flat_ids = expert_ids.reshape(-1)
    onehot = (flat_ids[:, None] == jnp.arange(experts, dtype=jnp.int32)[None, :]).astype(jnp.int32)
    earlier = jnp.sum((jnp.cumsum(onehot, axis=0) - onehot) * onehot, axis=1)
    slot_index = flat_ids * capacity + earlier
    source = (
        jnp.full((experts * capacity,), assign, jnp.int32)
        .at[slot_index]
        .set(jnp.arange(assign, dtype=jnp.int32))
    )
    token_of = source // choose_count
    zero_row = jnp.zeros((1, quarter), jnp.bfloat16)
    send_x = jnp.concatenate([tokens, zero_row], 0)[token_of].reshape(experts, capacity, quarter)
    slot_gate = jnp.concatenate([gate_weights.reshape(-1), jnp.zeros((1,), jnp.float32)], 0)[source]
    picked_dy = jnp.concatenate([cotangent, zero_row], 0)[token_of]
    send_dy = (
        (slot_gate[:, None] * picked_dy.astype(jnp.float32))
        .astype(jnp.bfloat16)
        .reshape(experts, capacity, quarter)
    )
    weight_in = w_in[0]
    weight_out = w_out[0]
    arrived_x = lax.all_to_all(send_x, "expert", split_axis=0, concat_axis=0, tiled=True)
    rows_x = arrived_x.reshape(-1, quarter)
    preact, activation = expert_hidden(rows_x, weight_in)
    out_rows = jnp.dot(activation, weight_out, preferred_element_type=jnp.float32).astype(
        jnp.bfloat16
    )
    rows_x, preact, activation, out_rows = (
        rows_x,
        preact,
        activation,
        out_rows.reshape(experts, capacity, quarter),
    )
    returned_out = lax.all_to_all(out_rows, "expert", split_axis=0, concat_axis=0, tiled=True)
    arrived_dy = lax.all_to_all(send_dy, "expert", split_axis=0, concat_axis=0, tiled=True)
    rows_dy = arrived_dy.reshape(-1, quarter)
    delta_hidden = expert_slope(rows_dy, weight_out, preact)
    out_grad = lax.dot_general(
        activation, rows_dy, (((0,), (0,)), ((), ())), preferred_element_type=jnp.float32
    ).astype(jnp.bfloat16)
    in_grad = lax.dot_general(
        rows_x, delta_hidden, (((0,), (0,)), ((), ())), preferred_element_type=jnp.float32
    ).astype(jnp.bfloat16)
    back_rows = lax.dot_general(
        delta_hidden, weight_in, (((1,), (1,)), ((), ())), preferred_element_type=jnp.float32
    ).astype(jnp.bfloat16)
    in_grad, out_grad, back_rows = (
        in_grad[None],
        out_grad[None],
        back_rows.reshape(experts, capacity, quarter),
    )
    returned_back = lax.all_to_all(back_rows, "expert", split_axis=0, concat_axis=0, tiled=True)

    def gather_rows(returned):
        flat_rows = returned.reshape(experts * capacity, quarter)
        return flat_rows[slot_index].astype(jnp.float32).reshape(tok_rows, choose_count, quarter)

    mixed_out = jnp.sum(gather_rows(returned_out) * gate_weights[:, :, None], axis=1).astype(
        jnp.bfloat16
    )
    token_grad = jnp.sum(gather_rows(returned_back), axis=1).astype(jnp.bfloat16)
    return (mixed_out, token_grad, in_grad, out_grad)


BF16, F32 = jnp.bfloat16, jnp.float32
MESH = pl.DeviceIdType.MESH


def mm(a, b, dims=((1,), (0,))):
    return lax.dot_general(a, b, (dims, ((), ())), preferred_element_type=F32)


def fused_kernel(
    n, cap,
    x_ref, dy_ref, meta_ref, win_ref, wout_ref,
    mixed_ref, tgrad_ref, ingrad_ref, outgrad_ref,
    xg, dyg, mg, rows_x, rows_dy, sel, selcat, gate, hp_s, hp_r, sp_s, sp_r, act, delta,
    ocat, osnd, bcat, bsnd, rso_s, rso_r, rsb_s, rsb_r,
    ring_s, ring_r, sib_s, sib_r, mring_s, mring_r, msib_s, msib_r,
    hx_s, hx_r, cx_s, cx_r, rs_s, rs_r,
):
    half = n // 2
    me = lax.axis_index("expert")
    dp_me = lax.axis_index("dp")
    core = me % 2
    chip = me // 2
    odd = chip % 2
    pos = (chip // 2) * (1 - 2 * odd) + odd * (n - 1)

    def device_at(p):
        hi = p // half
        return ((1 - hi) * 2 * p + hi * (2 * n - 1 - 2 * p)) * 2 + core

    right = {"expert": device_at((pos + 1) % n)}
    left = {"expert": device_at((pos + n - 1) % n)}
    sib = {"expert": me + 1 - 2 * core}
    peer = {"dp": 1 - dp_me}
    ring_to = (right, left)

    barrier = pltpu.get_barrier_semaphore()
    for d in (right, left, sib, peer):
        pl.semaphore_signal(barrier, inc=1, device_id=d, device_id_type=MESH)
    pl.semaphore_wait(barrier, 4)

    tok = x_ref.shape[0]
    hrow = tok // 2

    def rcopy(src, dst, ssem, rsem, dev):
        return pltpu.make_async_remote_copy(
            src_ref=src, dst_ref=dst, send_sem=ssem, recv_sem=rsem,
            device_id=dev, device_id_type=MESH,
        )

    pending = []

    def off(d, h):
        return (-h if d == 0 else h) % n

    def chunks_at(d, h):
        return (0, 1) if h < half else (d,)

    def ring_copy(t, d, h, c):
        own, buf = ((x_ref, xg), (dy_ref, dyg))[t]
        rows = pl.ds(c * hrow, hrow)
        src = own.at[rows] if h == 1 else buf.at[off(d, h - 1), 0, rows]
        return rcopy(src, buf.at[off(d, h), 0, rows], ring_s.at[t, d, h - 1, c], ring_r.at[t, d, h - 1, c], ring_to[d])

    def sib_copy(t, o):
        own, buf = ((x_ref, xg), (dy_ref, dyg))[t]
        src = own if o == 0 else buf.at[o, 0]
        return rcopy(src, buf.at[o, 1], sib_s.at[t, o], sib_r.at[t, o], sib)

    def meta_ring(d, h):
        src = meta_ref if h == 1 else mg.at[off(d, h - 1), 0]
        return rcopy(src, mg.at[off(d, h), 0], mring_s.at[d, h - 1], mring_r.at[d, h - 1], ring_to[d])

    def meta_sib(o):
        src = meta_ref if o == 0 else mg.at[o, 0]
        return rcopy(src, mg.at[o, 1], msib_s.at[o], msib_r.at[o], sib)

    def go(copy):
        copy.start()
        pending.append(copy)

    def send_first(t):
        if t == 0:
            for d in (0, 1):
                go(meta_ring(d, 1))
            go(meta_sib(0))
        for c in (0, 1):
            for d in (0, 1):
                go(ring_copy(t, d, 1, c))
        go(sib_copy(t, 0))

    def hop(t, h):
        if t == 0:
            for d in (0, 1):
                if h < half or d == 0:
                    meta_ring(d, h).wait_recv()
                    if h + 1 < half or (h + 1 == half and d == 0):
                        go(meta_ring(d, h + 1))
                    go(meta_sib(off(d, h)))
        for c in (0, 1):
            for d in (0, 1):
                if c in chunks_at(d, h):
                    ring_copy(t, d, h, c).wait_recv()
                    if h < half and c in chunks_at(d, h + 1):
                        go(ring_copy(t, d, h + 1, c))
        if h < half:
            for d in (0, 1):
                go(sib_copy(t, off(d, h)))
        else:
            go(sib_copy(t, half))

    before = (
        lax.broadcasted_iota(jnp.int32, (tok, tok), 0) < lax.broadcasted_iota(jnp.int32, (tok, tok), 1)
    ).astype(F32).astype(BF16)
    slot = lax.broadcasted_iota(jnp.int32, (cap, tok), 0).astype(F32)

    def routing(meta, expert):
        hit = (meta[0:8] == expert).astype(F32)
        g = jnp.sum(hit * meta[8:16], axis=0, keepdims=True)
        named = jnp.sum(hit, axis=0, keepdims=True)
        earlier = mm(jnp.broadcast_to(named, (8, tok)).astype(BF16), before)[0:1]
        chosen = jnp.where(earlier == slot, named, 0.0)
        return chosen.astype(BF16), jnp.sum(chosen * g, axis=1, keepdims=True)

    me_f = me.astype(F32)
    sib_f = (me + 1 - 2 * core).astype(F32)

    def span(o):
        return pl.ds(o * 2 * cap, 2 * cap)

    def take_x(o):
        sib_copy(0, o).wait_recv()
        meta_sib(o).wait_recv()
        for s in (0, 1):
            first = o == 0 and s == 0
            meta = meta_ref[...] if first else mg[o, s]
            block = x_ref[...] if first else xg[o, s]
            chosen, g = routing(meta, me_f)
            rows = pl.ds(o * 2 * cap + s * cap, cap)
            sel[rows] = chosen
            gate[rows] = g
            rows_x[rows] = mm(chosen, block).astype(BF16)
            if s == 0:
                selcat[pl.ds(o * 2 * cap, cap)] = chosen
                selcat[pl.ds(o * 2 * cap + cap, cap)] = routing(meta, sib_f)[0]
        hp_s[span(o)] = mm(rows_x[span(o)], win_ref[...]).astype(BF16)
        go(dp_copy(0, o))

    def dp_copy(t, o):
        s_buf, r_buf = ((hp_s, hp_r), (sp_s, sp_r))[t]
        return rcopy(s_buf.at[span(o)], r_buf.at[span(o)], hx_s.at[t, o], hx_r.at[t, o], peer)

    def take_dy(o):
        sib_copy(1, o).wait_recv()
        for s in (0, 1):
            rows = pl.ds(o * 2 * cap + s * cap, cap)
            block = dy_ref[...] if (o == 0 and s == 0) else dyg[o, s]
            rows_dy[rows] = (gate[rows] * mm(sel[rows], block)).astype(BF16)
        sp_s[span(o)] = mm(rows_dy[span(o)], wout_ref[...], ((1,), (1,))).astype(BF16)
        go(dp_copy(1, o))

    def cat_copy(t, o):
        s_buf, r_buf = ((osnd, ocat), (bsnd, bcat))[t]
        return rcopy(
            s_buf.at[pl.ds(o * cap, cap)], r_buf.at[pl.ds(o * 2 * cap + cap, cap)],
            cx_s.at[t, o], cx_r.at[t, o], sib,
        )

    def hidden_of(o):
        return hp_s[span(o)].astype(F32) + hp_r[span(o)].astype(F32)

    def give(t, o, rows):
        s_buf, r_buf = ((osnd, ocat), (bsnd, bcat))[t]
        r_buf[pl.ds(o * 2 * cap, cap)] = rows[:cap]
        s_buf[pl.ds(o * cap, cap)] = rows[cap:]
        go(cat_copy(t, o))

    def forward(o):
        dp_copy(0, o).wait_recv()
        activation = jax.nn.silu(hidden_of(o)).astype(BF16)
        act[span(o)] = activation
        out_rows = mm(activation, wout_ref[...]).astype(BF16)
        give(0, o, (gate[span(o)] * out_rows.astype(F32)).astype(BF16))

    def backward(o):
        dp_copy(1, o).wait_recv()
        slope = sp_s[span(o)].astype(F32) + sp_r[span(o)].astype(F32)
        d_hidden = (slope * silu_slope(hidden_of(o))).astype(BF16)
        delta[span(o)] = d_hidden
        give(1, o, mm(d_hidden, win_ref[...], ((1,), (1,))).astype(BF16))

    def contribution(t, o, c):
        buf = (ocat, bcat)[t]
        return mm(selcat[span(o), c * hrow:(c + 1) * hrow], buf[span(o)], ((0,), (0,)))

    def rs_copy(t, d, h, c):
        s_buf, r_buf = ((rso_s, rso_r), (rsb_s, rsb_r))[t]
        rows = pl.ds(c * hrow, hrow)
        return rcopy(
            s_buf.at[d, h - 1, rows], r_buf.at[d, h - 1, rows],
            rs_s.at[t, d, h - 1, c], rs_r.at[t, d, h - 1, c], ring_to[d],
        )

    def rs_hop(t, h):
        s_buf, r_buf = ((rso_s, rso_r), (rsb_s, rsb_r))[t]
        for o in {off(1, h), off(0, h)}:
            cat_copy(t, o).wait_recv()
        for c in (0, 1):
            for d in (0, 1):
                if c not in chunks_at(d, h):
                    continue
                rows = pl.ds(c * hrow, hrow)
                total = contribution(t, off(1 - d, h), c)
                if h < half and c in chunks_at(d, h + 1):
                    rs_copy(t, d, h + 1, c).wait_recv()
                    total = total + r_buf[d, h, rows].astype(F32)
                s_buf[d, h - 1, rows] = total.astype(BF16)
                go(rs_copy(t, d, h, c))

    def rs_last(t):
        r_buf = (rso_r, rsb_r)[t]
        out = (mixed_ref, tgrad_ref)[t]
        cat_copy(t, 0).wait_recv()
        for c in (0, 1):
            rows = pl.ds(c * hrow, hrow)
            total = contribution(t, 0, c)
            for d in (0, 1):
                rs_copy(t, d, 1, c).wait_recv()
                total = total + r_buf[d, 0, rows].astype(F32)
            out[rows] = total.astype(BF16)

    def out_grad():
        f_hidden = act.shape[1]
        tile = 256 if f_hidden % 256 == 0 else f_hidden

        @pl.loop(0, f_hidden // tile)
        def _(i):
            cols = pl.ds(pl.multiple_of(i * tile, tile), tile)
            outgrad_ref[cols] = mm(act[:, cols], rows_dy[...], ((0,), (0,))).astype(BF16)

    def in_grad():
        width = rows_x.shape[1]
        tile = 256 if width % 256 == 0 else width

        @pl.loop(0, width // tile)
        def _(i):
            cols = pl.ds(pl.multiple_of(i * tile, tile), tile)
            ingrad_ref[cols] = mm(rows_x[:, cols], delta[...], ((0,), (0,))).astype(BF16)

    order = [[0]] + [[off(0, h), off(1, h)] for h in range(1, half)] + [[half]]
    send_first(0)
    for h in range(1, half):
        hop(0, h)
        for o in order[h - 1]:
            take_x(o)
    send_first(1)
    hop(0, half)
    for o in order[half - 1]:
        take_x(o)
    hop(1, 1)
    take_x(half)
    for h in range(2, half):
        hop(1, h)
        for o in order[h - 2]:
            take_dy(o)
            forward(o)
    hop(1, half)
    for i in (half - 2, half - 1, half):
        for o in order[i]:
            take_dy(o)
    for i in (half, half - 1, half - 2):
        for o in order[i]:
            forward(o)
    for h in range(half, 0, -1):
        rs_hop(0, h)
        for o in order[half - h]:
            backward(o)
    for o in order[half]:
        backward(o)
    rs_hop(1, half)
    rs_last(0)
    for h in range(half - 1, 0, -1):
        rs_hop(1, h)
        if h == half - 1:
            out_grad()
        if h == half - 2:
            in_grad()
    rs_last(1)
    for copy in pending:
        copy.wait_send()


def local_fused(tokens, cotangent, expert_ids, gate_weights, w_in, w_out):
    experts = lax.axis_size("expert")
    tok_rows, width = tokens.shape
    top = expert_ids.shape[1]
    hid = w_in.shape[2]
    cap = max(2, 4 * tok_rows * top // (3 * experts))
    n = experts // 2
    half = n // 2
    slots = experts * cap
    pad = 8 - top
    meta = jnp.concatenate(
        [
            jnp.pad(expert_ids.T.astype(F32), ((0, pad), (0, 0)), constant_values=-1.0),
            jnp.pad(gate_weights.T, ((0, pad), (0, 0))),
        ],
        0,
    )
    vm = pltpu.VMEM
    dma = pltpu.SemaphoreType.DMA
    mixed, tgrad, ingrad, outgrad = pl.pallas_call(
        functools.partial(fused_kernel, n, cap),
        out_shape=(
            jax.ShapeDtypeStruct((tok_rows, width), BF16),
            jax.ShapeDtypeStruct((tok_rows, width), BF16),
            jax.ShapeDtypeStruct((width, hid), BF16),
            jax.ShapeDtypeStruct((hid, width), BF16),
        ),
        in_specs=[pl.BlockSpec(memory_space=pltpu.VMEM)] * 5,
        out_specs=[pl.BlockSpec(memory_space=pltpu.VMEM)] * 4,
        scratch_shapes=[
            vm((n, 2, tok_rows, width), BF16),
            vm((n, 2, tok_rows, width), BF16),
            vm((n, 2, 16, tok_rows), F32),
            vm((slots, width), BF16),
            vm((slots, width), BF16),
            vm((slots, tok_rows), BF16),
            vm((slots, tok_rows), BF16),
            vm((slots, 1), F32),
            vm((slots, hid), BF16),
            vm((slots, hid), BF16),
            vm((slots, hid), BF16),
            vm((slots, hid), BF16),
            vm((slots, hid), BF16),
            vm((slots, hid), BF16),
            vm((slots, width), BF16),
            vm((slots // 2, width), BF16),
            vm((slots, width), BF16),
            vm((slots // 2, width), BF16),
            vm((2, half, tok_rows, width), BF16),
            vm((2, half, tok_rows, width), BF16),
            vm((2, half, tok_rows, width), BF16),
            vm((2, half, tok_rows, width), BF16),
            dma((2, 2, half, 2)),
            dma((2, 2, half, 2)),
            dma((2, n)),
            dma((2, n)),
            dma((2, half)),
            dma((2, half)),
            dma((n,)),
            dma((n,)),
            dma((2, n)),
            dma((2, n)),
            dma((2, n)),
            dma((2, n)),
            dma((2, 2, half, 2)),
            dma((2, 2, half, 2)),
        ],
        compiler_params=pltpu.CompilerParams(
            collective_id=0, has_side_effects=True, vmem_limit_bytes=67043328
        ),
        name="fused_experts",
    )(tokens, cotangent, meta, w_in[0], w_out[0])
    return (mixed, tgrad, ingrad[None], outgrad[None])


def gathers_pay(mesh, tok_rows, top):
    experts = mesh.shape["expert"]
    cap = max(2, 4 * tok_rows * top // (3 * experts))
    return (
        mesh.shape["dp"] == 2
        and experts % 8 == 0
        and top <= 8
        and tok_rows % 128 == 0
        and cap % 16 == 0
        and tok_rows <= 2 * cap
    )


def solution(mesh):
    in_specs = (
        P("expert", "dp"),
        P("expert", "dp"),
        P("expert", None),
        P("expert", None),
        P("expert", "dp", None),
        P("expert", None, "dp"),
    )
    out_specs = (
        P("expert", "dp"),
        P("expert", "dp"),
        P("expert", "dp", None),
        P("expert", None, "dp"),
    )

    def run(tokens, cotangent, expert_ids, gate_weights, w_in, w_out):
        rows, top = expert_ids.shape
        fused = gathers_pay(mesh, rows // mesh.shape["expert"], top)
        body = jax.shard_map(
            local_fused if fused else local_slots,
            mesh=mesh, in_specs=in_specs, out_specs=out_specs, check_vma=False,
        )
        return body(tokens, cotangent, expert_ids, gate_weights, w_in, w_out)

    return run
```

```python
import functools

import jax
import jax.numpy as jnp
from jax import lax
from jax.experimental import pallas as pl
from jax.experimental.pallas import tpu as pltpu
from jax.sharding import PartitionSpec as P


def silu_slope(hidden_value):
    logistic = jax.nn.sigmoid(hidden_value)
    return logistic * (1.0 + hidden_value * (1.0 - logistic))


def expert_hidden(rows_x, weight_in):
    partial_sum = jnp.dot(rows_x, weight_in, preferred_element_type=jnp.float32)
    share_sum = lax.psum_scatter(
        partial_sum.astype(jnp.bfloat16), "dp", scatter_dimension=1, tiled=True
    ).astype(jnp.float32)
    share_act = jax.nn.silu(share_sum).astype(jnp.bfloat16)
    return (share_sum, lax.all_gather(share_act, "dp", axis=1, tiled=True))


def expert_slope(rows_dy, weight_out, preact):
    partial_sum = lax.dot_general(
        rows_dy, weight_out, (((1,), (1,)), ((), ())), preferred_element_type=jnp.float32
    )
    share_sum = lax.psum_scatter(
        partial_sum.astype(jnp.bfloat16), "dp", scatter_dimension=1, tiled=True
    ).astype(jnp.float32)
    share_delta = (share_sum * silu_slope(preact)).astype(jnp.bfloat16)
    return lax.all_gather(share_delta, "dp", axis=1, tiled=True)


def local_slots(tokens, cotangent, expert_ids, gate_weights, w_in, w_out):
    experts = lax.axis_size("expert")
    tok_rows, quarter = tokens.shape
    choose_count = expert_ids.shape[1]
    capacity = max(2, 4 * tok_rows * choose_count // (3 * experts))
    assign = tok_rows * choose_count
    flat_ids = expert_ids.reshape(-1)
    onehot = (flat_ids[:, None] == jnp.arange(experts, dtype=jnp.int32)[None, :]).astype(jnp.int32)
    earlier = jnp.sum((jnp.cumsum(onehot, axis=0) - onehot) * onehot, axis=1)
    slot_index = flat_ids * capacity + earlier
    source = (
        jnp.full((experts * capacity,), assign, jnp.int32)
        .at[slot_index]
        .set(jnp.arange(assign, dtype=jnp.int32))
    )
    token_of = source // choose_count
    zero_row = jnp.zeros((1, quarter), jnp.bfloat16)
    send_x = jnp.concatenate([tokens, zero_row], 0)[token_of].reshape(experts, capacity, quarter)
    slot_gate = jnp.concatenate([gate_weights.reshape(-1), jnp.zeros((1,), jnp.float32)], 0)[source]
    picked_dy = jnp.concatenate([cotangent, zero_row], 0)[token_of]
    send_dy = (
        (slot_gate[:, None] * picked_dy.astype(jnp.float32))
        .astype(jnp.bfloat16)
        .reshape(experts, capacity, quarter)
    )
    weight_in = w_in[0]
    weight_out = w_out[0]
    arrived_x = lax.all_to_all(send_x, "expert", split_axis=0, concat_axis=0, tiled=True)
    rows_x = arrived_x.reshape(-1, quarter)
    preact, activation = expert_hidden(rows_x, weight_in)
    out_rows = jnp.dot(activation, weight_out, preferred_element_type=jnp.float32).astype(
        jnp.bfloat16
    )
    rows_x, preact, activation, out_rows = (
        rows_x,
        preact,
        activation,
        out_rows.reshape(experts, capacity, quarter),
    )
    returned_out = lax.all_to_all(out_rows, "expert", split_axis=0, concat_axis=0, tiled=True)
    arrived_dy = lax.all_to_all(send_dy, "expert", split_axis=0, concat_axis=0, tiled=True)
    rows_dy = arrived_dy.reshape(-1, quarter)
    delta_hidden = expert_slope(rows_dy, weight_out, preact)
    out_grad = lax.dot_general(
        activation, rows_dy, (((0,), (0,)), ((), ())), preferred_element_type=jnp.float32
    ).astype(jnp.bfloat16)
    in_grad = lax.dot_general(
        rows_x, delta_hidden, (((0,), (0,)), ((), ())), preferred_element_type=jnp.float32
    ).astype(jnp.bfloat16)
    back_rows = lax.dot_general(
        delta_hidden, weight_in, (((1,), (1,)), ((), ())), preferred_element_type=jnp.float32
    ).astype(jnp.bfloat16)
    in_grad, out_grad, back_rows = (
        in_grad[None],
        out_grad[None],
        back_rows.reshape(experts, capacity, quarter),
    )
    returned_back = lax.all_to_all(back_rows, "expert", split_axis=0, concat_axis=0, tiled=True)

    def gather_rows(returned):
        flat_rows = returned.reshape(experts * capacity, quarter)
        return flat_rows[slot_index].astype(jnp.float32).reshape(tok_rows, choose_count, quarter)

    mixed_out = jnp.sum(gather_rows(returned_out) * gate_weights[:, :, None], axis=1).astype(
        jnp.bfloat16
    )
    token_grad = jnp.sum(gather_rows(returned_back), axis=1).astype(jnp.bfloat16)
    return (mixed_out, token_grad, in_grad, out_grad)


BF16, F32 = jnp.bfloat16, jnp.float32
MESH = pl.DeviceIdType.MESH


def mm(a, b, dims=((1,), (0,))):
    return lax.dot_general(a, b, (dims, ((), ())), preferred_element_type=F32)


def fused_kernel(
    n, cap,
    x_ref, dy_ref, ids_ref, gates_ref, win_hbm, wout_hbm,
    mixed_ref, tgrad_ref, ingrad_hbm, outgrad_hbm,
    win_ref, wout_ref, ingrad_ref, outgrad_ref, meta_ref,
    xg, dyg, mg, rows_x, rows_dy, sel, selcat, gate, hp_s, hp_r, sp_s, sp_r, act, delta,
    ocat, osnd, bcat, bsnd, rso_s, rso_r, rsb_s, rsb_r,
    ring_s, ring_r, sib_s, sib_r, mring_s, mring_r, msib_s, msib_r,
    hx_s, hx_r, cx_s, cx_r, rs_s, rs_r, load_sem, ig_sem, og_sem,
):
    half = n // 2
    me = lax.axis_index("expert")
    dp_me = lax.axis_index("dp")
    core = me % 2
    chip = me // 2
    odd = chip % 2
    pos = (chip // 2) * (1 - 2 * odd) + odd * (n - 1)

    def device_at(p):
        hi = p // half
        return ((1 - hi) * 2 * p + hi * (2 * n - 1 - 2 * p)) * 2 + core

    right = {"expert": device_at((pos + 1) % n)}
    left = {"expert": device_at((pos + n - 1) % n)}
    sib = {"expert": me + 1 - 2 * core}
    peer = {"dp": 1 - dp_me}
    ring_to = (right, left)

    load_in = pltpu.make_async_copy(win_hbm, win_ref, load_sem.at[0])
    load_out = pltpu.make_async_copy(wout_hbm, wout_ref, load_sem.at[1])
    load_in.start()
    load_out.start()

    barrier = pltpu.get_barrier_semaphore()
    for d in (right, left, sib, peer):
        pl.semaphore_signal(barrier, inc=1, device_id=d, device_id_type=MESH)
    pl.semaphore_wait(barrier, 4)

    tok = x_ref.shape[0]
    hrow = tok // 2

    def rcopy(src, dst, ssem, rsem, dev):
        return pltpu.make_async_remote_copy(
            src_ref=src, dst_ref=dst, send_sem=ssem, recv_sem=rsem,
            device_id=dev, device_id_type=MESH,
        )

    pending = []

    def off(d, h):
        return (-h if d == 0 else h) % n

    def chunks_at(d, h):
        return (0, 1) if h < half else (d,)

    def ring_copy(t, d, h, c):
        own, buf = ((x_ref, xg), (dy_ref, dyg))[t]
        rows = pl.ds(c * hrow, hrow)
        src = own.at[rows] if h == 1 else buf.at[off(d, h - 1), 0, rows]
        return rcopy(src, buf.at[off(d, h), 0, rows], ring_s.at[t, d, h - 1, c], ring_r.at[t, d, h - 1, c], ring_to[d])

    def sib_copy(t, o, c):
        own, buf = ((x_ref, xg), (dy_ref, dyg))[t]
        rows = pl.ds(c * hrow, hrow)
        src = own.at[rows] if o == 0 else buf.at[o, 0, rows]
        return rcopy(src, buf.at[o, 1, rows], sib_s.at[t, o, c], sib_r.at[t, o, c], sib)

    def meta_ring(d, h):
        src = meta_ref if h == 1 else mg.at[off(d, h - 1), 0]
        return rcopy(src, mg.at[off(d, h), 0], mring_s.at[d, h - 1], mring_r.at[d, h - 1], ring_to[d])

    def meta_sib(o):
        src = meta_ref if o == 0 else mg.at[o, 0]
        return rcopy(src, mg.at[o, 1], msib_s.at[o], msib_r.at[o], sib)

    def go(copy):
        copy.start()
        pending.append(copy)

    def send_first(t):
        for c in (0, 1):
            for d in (0, 1):
                go(ring_copy(t, d, 1, c))
        for c in (0, 1):
            go(sib_copy(t, 0, c))

    def send_meta():
        top = ids_ref.shape[0]
        meta_ref[...] = jnp.full(meta_ref.shape, -1.0, F32)
        meta_ref[0:top] = ids_ref[...].astype(F32)
        meta_ref[8:8 + top] = gates_ref[...]
        for d in (0, 1):
            go(meta_ring(d, 1))
        go(meta_sib(0))

    def hop(t, h):
        if t == 0:
            for d in (0, 1):
                if h < half or d == 0:
                    meta_ring(d, h).wait_recv()
                    if h + 1 < half or (h + 1 == half and d == 0):
                        go(meta_ring(d, h + 1))
                    go(meta_sib(off(d, h)))
        for c in (0, 1):
            for d in (0, 1):
                if c in chunks_at(d, h):
                    ring_copy(t, d, h, c).wait_recv()
                    if h < half and c in chunks_at(d, h + 1):
                        go(ring_copy(t, d, h + 1, c))
                    go(sib_copy(t, off(d, h), c))

    def sib_arrived(t, o):
        for c in (0, 1):
            sib_copy(t, o, c).wait_recv()

    before = (
        lax.broadcasted_iota(jnp.int32, (tok, tok), 0) < lax.broadcasted_iota(jnp.int32, (tok, tok), 1)
    ).astype(F32).astype(BF16)
    slot = lax.broadcasted_iota(jnp.int32, (cap, tok), 0).astype(F32)

    def routing(meta, expert):
        hit = (meta[0:8] == expert).astype(F32)
        g = jnp.sum(hit * meta[8:16], axis=0, keepdims=True)
        named = jnp.sum(hit, axis=0, keepdims=True)
        earlier = mm(jnp.broadcast_to(named, (8, tok)).astype(BF16), before)[0:1]
        chosen = jnp.where(earlier == slot, named, 0.0)
        return chosen.astype(BF16), jnp.sum(chosen * g, axis=1, keepdims=True)

    me_f = me.astype(F32)
    sib_f = (me + 1 - 2 * core).astype(F32)

    def span(o):
        return pl.ds(o * 2 * cap, 2 * cap)

    def take_x(o):
        sib_arrived(0, o)
        meta_sib(o).wait_recv()
        for s in (0, 1):
            first = o == 0 and s == 0
            meta = meta_ref[...] if first else mg[o, s]
            block = x_ref[...] if first else xg[o, s]
            chosen, g = routing(meta, me_f)
            rows = pl.ds(o * 2 * cap + s * cap, cap)
            sel[rows] = chosen
            gate[rows] = g
            rows_x[rows] = mm(chosen, block).astype(BF16)
            if s == 0:
                selcat[pl.ds(o * 2 * cap, cap)] = chosen
                selcat[pl.ds(o * 2 * cap + cap, cap)] = routing(meta, sib_f)[0]
        hp_s[span(o)] = mm(rows_x[span(o)], win_ref[...]).astype(BF16)
        go(dp_copy(0, o))

    def dp_copy(t, o):
        s_buf, r_buf = ((hp_s, hp_r), (sp_s, sp_r))[t]
        return rcopy(s_buf.at[span(o)], r_buf.at[span(o)], hx_s.at[t, o], hx_r.at[t, o], peer)

    def take_dy(o):
        sib_arrived(1, o)
        for s in (0, 1):
            rows = pl.ds(o * 2 * cap + s * cap, cap)
            block = dy_ref[...] if (o == 0 and s == 0) else dyg[o, s]
            rows_dy[rows] = (gate[rows] * mm(sel[rows], block)).astype(BF16)
        sp_s[span(o)] = mm(rows_dy[span(o)], wout_ref[...], ((1,), (1,))).astype(BF16)
        go(dp_copy(1, o))

    def cat_copy(t, o):
        s_buf, r_buf = ((osnd, ocat), (bsnd, bcat))[t]
        return rcopy(
            s_buf.at[pl.ds(o * cap, cap)], r_buf.at[pl.ds(o * 2 * cap + cap, cap)],
            cx_s.at[t, o], cx_r.at[t, o], sib,
        )

    def hidden_of(o):
        return hp_s[span(o)].astype(F32) + hp_r[span(o)].astype(F32)

    def give(t, o, rows):
        s_buf, r_buf = ((osnd, ocat), (bsnd, bcat))[t]
        r_buf[pl.ds(o * 2 * cap, cap)] = rows[:cap]
        s_buf[pl.ds(o * cap, cap)] = rows[cap:]
        go(cat_copy(t, o))

    def forward(o):
        dp_copy(0, o).wait_recv()
        activation = jax.nn.silu(hidden_of(o)).astype(BF16)
        act[span(o)] = activation
        out_rows = mm(activation, wout_ref[...]).astype(BF16)
        give(0, o, (gate[span(o)] * out_rows.astype(F32)).astype(BF16))

    def backward(o):
        dp_copy(1, o).wait_recv()
        slope = sp_s[span(o)].astype(F32) + sp_r[span(o)].astype(F32)
        d_hidden = (slope * silu_slope(hidden_of(o))).astype(BF16)
        delta[span(o)] = d_hidden
        give(1, o, mm(d_hidden, win_ref[...], ((1,), (1,))).astype(BF16))

    def contribution(t, o, c):
        buf = (ocat, bcat)[t]
        return mm(selcat[span(o), c * hrow:(c + 1) * hrow], buf[span(o)], ((0,), (0,)))

    def rs_copy(t, d, h, c):
        s_buf, r_buf = ((rso_s, rso_r), (rsb_s, rsb_r))[t]
        rows = pl.ds(c * hrow, hrow)
        return rcopy(
            s_buf.at[d, h - 1, rows], r_buf.at[d, h - 1, rows],
            rs_s.at[t, d, h - 1, c], rs_r.at[t, d, h - 1, c], ring_to[d],
        )

    def rs_hop(t, h):
        s_buf, r_buf = ((rso_s, rso_r), (rsb_s, rsb_r))[t]
        for o in {off(1, h), off(0, h)}:
            cat_copy(t, o).wait_recv()
        for late in (0, 1):
            for d in (0, 1):
                c = d if late else 1 - d
                if c not in chunks_at(d, h):
                    continue
                rows = pl.ds(c * hrow, hrow)
                total = contribution(t, off(1 - d, h), c)
                if h < half and c in chunks_at(d, h + 1):
                    rs_copy(t, d, h + 1, c).wait_recv()
                    total = total + r_buf[d, h, rows].astype(F32)
                s_buf[d, h - 1, rows] = total.astype(BF16)
                go(rs_copy(t, d, h, c))

    def rs_last(t):
        r_buf = (rso_r, rsb_r)[t]
        out = (mixed_ref, tgrad_ref)[t]
        cat_copy(t, 0).wait_recv()
        for c in (0, 1):
            rows = pl.ds(c * hrow, hrow)
            total = contribution(t, 0, c)
            for d in (0, 1):
                rs_copy(t, d, 1, c).wait_recv()
                total = total + r_buf[d, 0, rows].astype(F32)
            out[rows] = total.astype(BF16)

    def grad_tile(i, left, right, v_ref, hbm, sem):
        cols = slice(i * tile, (i + 1) * tile)
        v_ref[cols] = mm(left[:, cols], right[...], ((0,), (0,))).astype(BF16)
        copy = pltpu.make_async_copy(v_ref.at[cols], hbm.at[cols], sem.at[i])
        copy.start()
        stores.append(copy)

    def out_tiles(tiles):
        for i in tiles:
            grad_tile(i, act, rows_dy, outgrad_ref, outgrad_hbm, og_sem)

    def in_tiles(tiles):
        for i in tiles:
            grad_tile(i, rows_x, delta, ingrad_ref, ingrad_hbm, ig_sem)

    stores = []
    tile = 256
    n_out, n_in = act.shape[1] // tile, rows_x.shape[1] // tile

    def part(count, h):
        k = half - 1 - h
        return range(count * k // (half - 1), count * (k + 1) // (half - 1))

    order = [[0]] + [[off(0, h), off(1, h)] for h in range(1, half)] + [[half]]

    def each(f, i):
        for o in order[i]:
            f(o)

    send_first(0)
    send_meta()
    load_in.wait()
    take_x(0)
    for h in range(1, half):
        hop(0, h)
        if h == half - 1:
            send_first(1)
            load_out.wait()
        each(take_x, h)
    hop(0, half)
    take_x(half)
    for h in range(1, half - 1):
        hop(1, h)
        each(take_dy, h - 1)
        each(forward, h - 1)
    hop(1, half - 1)
    each(take_dy, half - 2)
    each(forward, half - 2)
    each(forward, half)
    each(forward, half - 1)
    rs_hop(0, half)
    hop(1, half)
    each(take_dy, half - 1)
    rs_hop(0, half - 1)
    each(take_dy, half)
    each(backward, 0)
    out_tiles(part(n_out, half - 1))
    for h in range(half - 2, 0, -1):
        rs_hop(0, h)
        each(backward, half - 1 - h)
        out_tiles(part(n_out, h))
    each(backward, half - 1)
    each(backward, half)
    rs_hop(1, half)
    rs_last(0)
    for h in range(half - 1, 0, -1):
        rs_hop(1, h)
        in_tiles(part(n_in, h))
    rs_last(1)
    for copy in stores:
        copy.wait()
    for copy in pending:
        copy.wait_send()


def copy_kernel(count, *refs):
    srcs, dsts, bufs = refs[:count], refs[count:2 * count], refs[2 * count:3 * count]
    in_sem, out_sem = refs[3 * count:]
    into, outof = [], []
    for j in range(count):
        rows = srcs[j].shape[0] // 4
        for q in range(4):
            at = pl.ds(q * rows, rows)
            into.append(pltpu.make_async_copy(srcs[j].at[at], bufs[j].at[at], in_sem.at[j, q]))
            outof.append(pltpu.make_async_copy(bufs[j].at[at], dsts[j].at[at], out_sem.at[j, q]))
    for copy in into:
        copy.start()
    for a, b in zip(into, outof):
        a.wait()
        b.start()
    for copy in outof:
        copy.wait()


def settle(arrays):
    count = len(arrays)
    return pl.pallas_call(
        functools.partial(copy_kernel, count),
        out_shape=[jax.ShapeDtypeStruct(a.shape, a.dtype) for a in arrays],
        in_specs=[pl.BlockSpec(memory_space=pl.ANY)] * count,
        out_specs=[pl.BlockSpec(memory_space=pl.ANY)] * count,
        scratch_shapes=[pltpu.VMEM(a.shape, a.dtype) for a in arrays]
        + [pltpu.SemaphoreType.DMA((count, 4))] * 2,
        name="settle",
    )(*arrays)


def local_fused(tokens, cotangent, expert_ids, gate_weights, w_in, w_out):
    experts = lax.axis_size("expert")
    tok_rows, width = tokens.shape
    top = expert_ids.shape[1]
    hid = w_in.shape[2]
    cap = max(2, 4 * tok_rows * top // (3 * experts))
    n = experts // 2
    half = n // 2
    slots = experts * cap
    vm = pltpu.VMEM
    dma = pltpu.SemaphoreType.DMA
    mixed, tgrad, ingrad, outgrad = pl.pallas_call(
        functools.partial(fused_kernel, n, cap),
        out_shape=(
            jax.ShapeDtypeStruct((tok_rows, width), BF16),
            jax.ShapeDtypeStruct((tok_rows, width), BF16),
            jax.ShapeDtypeStruct((width, hid), BF16),
            jax.ShapeDtypeStruct((hid, width), BF16),
        ),
        in_specs=[pl.BlockSpec(memory_space=pltpu.VMEM)] * 4 + [pl.BlockSpec(memory_space=pl.ANY)] * 2,
        out_specs=[pl.BlockSpec(memory_space=pltpu.VMEM)] * 2 + [pl.BlockSpec(memory_space=pl.ANY)] * 2,
        scratch_shapes=[
            vm((width, hid), BF16),
            vm((hid, width), BF16),
            vm((width, hid), BF16),
            vm((hid, width), BF16),
            vm((16, tok_rows), F32),
            vm((n, 2, tok_rows, width), BF16),
            vm((n, 2, tok_rows, width), BF16),
            vm((n, 2, 16, tok_rows), F32),
            vm((slots, width), BF16),
            vm((slots, width), BF16),
            vm((slots, tok_rows), BF16),
            vm((slots, tok_rows), BF16),
            vm((slots, 1), F32),
            vm((slots, hid), BF16),
            vm((slots, hid), BF16),
            vm((slots, hid), BF16),
            vm((slots, hid), BF16),
            vm((slots, hid), BF16),
            vm((slots, hid), BF16),
            vm((slots, width), BF16),
            vm((slots // 2, width), BF16),
            vm((slots, width), BF16),
            vm((slots // 2, width), BF16),
            vm((2, half, tok_rows, width), BF16),
            vm((2, half, tok_rows, width), BF16),
            vm((2, half, tok_rows, width), BF16),
            vm((2, half, tok_rows, width), BF16),
            dma((2, 2, half, 2)),
            dma((2, 2, half, 2)),
            dma((2, n, 2)),
            dma((2, n, 2)),
            dma((2, half)),
            dma((2, half)),
            dma((n,)),
            dma((n,)),
            dma((2, n)),
            dma((2, n)),
            dma((2, n)),
            dma((2, n)),
            dma((2, 2, half, 2)),
            dma((2, 2, half, 2)),
            dma((2,)),
            dma((width // 256,)),
            dma((hid // 256,)),
        ],
        compiler_params=pltpu.CompilerParams(
            collective_id=0, has_side_effects=True, vmem_limit_bytes=67043328
        ),
        name="fused_experts",
    )(tokens, cotangent, expert_ids.T, gate_weights.T, w_in[0], w_out[0])
    mixed, tgrad, ingrad, outgrad = settle([mixed, tgrad, ingrad, outgrad])
    return (mixed, tgrad, ingrad[None], outgrad[None])


def gathers_pay(mesh, tok_rows, top, width, hid):
    experts = mesh.shape["expert"]
    cap = max(2, 4 * tok_rows * top // (3 * experts))
    return (
        mesh.shape["dp"] == 2
        and experts % 8 == 0
        and top <= 8
        and tok_rows % 128 == 0
        and cap % 16 == 0
        and tok_rows <= 2 * cap
        and width % 256 == 0
        and hid % 256 == 0
    )


def solution(mesh):
    in_specs = (
        P("expert", "dp"),
        P("expert", "dp"),
        P("expert", None),
        P("expert", None),
        P("expert", "dp", None),
        P("expert", None, "dp"),
    )
    out_specs = (
        P("expert", "dp"),
        P("expert", "dp"),
        P("expert", "dp", None),
        P("expert", None, "dp"),
    )

    def run(tokens, cotangent, expert_ids, gate_weights, w_in, w_out):
        rows, top = expert_ids.shape
        width = tokens.shape[1] // mesh.shape["dp"]
        fused = gathers_pay(mesh, rows // mesh.shape["expert"], top, width, w_in.shape[2])
        body = jax.shard_map(
            local_fused if fused else local_slots,
            mesh=mesh, in_specs=in_specs, out_specs=out_specs, check_vma=False,
        )
        return body(tokens, cotangent, expert_ids, gate_weights, w_in, w_out)

    return run
```

```python
import functools

import jax
import jax.numpy as jnp
from jax import lax
from jax.experimental import pallas as pl
from jax.experimental.pallas import tpu as pltpu
from jax.sharding import PartitionSpec as P


def silu_slope(hidden_value):
    logistic = jax.nn.sigmoid(hidden_value)
    return logistic * (1.0 + hidden_value * (1.0 - logistic))


def expert_hidden(rows_x, weight_in):
    partial_sum = jnp.dot(rows_x, weight_in, preferred_element_type=jnp.float32)
    share_sum = lax.psum_scatter(
        partial_sum.astype(jnp.bfloat16), "dp", scatter_dimension=1, tiled=True
    ).astype(jnp.float32)
    share_act = jax.nn.silu(share_sum).astype(jnp.bfloat16)
    return (share_sum, lax.all_gather(share_act, "dp", axis=1, tiled=True))


def expert_slope(rows_dy, weight_out, preact):
    partial_sum = lax.dot_general(
        rows_dy, weight_out, (((1,), (1,)), ((), ())), preferred_element_type=jnp.float32
    )
    share_sum = lax.psum_scatter(
        partial_sum.astype(jnp.bfloat16), "dp", scatter_dimension=1, tiled=True
    ).astype(jnp.float32)
    share_delta = (share_sum * silu_slope(preact)).astype(jnp.bfloat16)
    return lax.all_gather(share_delta, "dp", axis=1, tiled=True)


def local_slots(tokens, cotangent, expert_ids, gate_weights, w_in, w_out):
    experts = lax.axis_size("expert")
    tok_rows, quarter = tokens.shape
    choose_count = expert_ids.shape[1]
    capacity = max(2, 4 * tok_rows * choose_count // (3 * experts))
    assign = tok_rows * choose_count
    flat_ids = expert_ids.reshape(-1)
    onehot = (flat_ids[:, None] == jnp.arange(experts, dtype=jnp.int32)[None, :]).astype(jnp.int32)
    earlier = jnp.sum((jnp.cumsum(onehot, axis=0) - onehot) * onehot, axis=1)
    slot_index = flat_ids * capacity + earlier
    source = (
        jnp.full((experts * capacity,), assign, jnp.int32)
        .at[slot_index]
        .set(jnp.arange(assign, dtype=jnp.int32))
    )
    token_of = source // choose_count
    zero_row = jnp.zeros((1, quarter), jnp.bfloat16)
    send_x = jnp.concatenate([tokens, zero_row], 0)[token_of].reshape(experts, capacity, quarter)
    slot_gate = jnp.concatenate([gate_weights.reshape(-1), jnp.zeros((1,), jnp.float32)], 0)[source]
    picked_dy = jnp.concatenate([cotangent, zero_row], 0)[token_of]
    send_dy = (
        (slot_gate[:, None] * picked_dy.astype(jnp.float32))
        .astype(jnp.bfloat16)
        .reshape(experts, capacity, quarter)
    )
    weight_in = w_in[0]
    weight_out = w_out[0]
    arrived_x = lax.all_to_all(send_x, "expert", split_axis=0, concat_axis=0, tiled=True)
    rows_x = arrived_x.reshape(-1, quarter)
    preact, activation = expert_hidden(rows_x, weight_in)
    out_rows = jnp.dot(activation, weight_out, preferred_element_type=jnp.float32).astype(
        jnp.bfloat16
    )
    rows_x, preact, activation, out_rows = (
        rows_x,
        preact,
        activation,
        out_rows.reshape(experts, capacity, quarter),
    )
    returned_out = lax.all_to_all(out_rows, "expert", split_axis=0, concat_axis=0, tiled=True)
    arrived_dy = lax.all_to_all(send_dy, "expert", split_axis=0, concat_axis=0, tiled=True)
    rows_dy = arrived_dy.reshape(-1, quarter)
    delta_hidden = expert_slope(rows_dy, weight_out, preact)
    out_grad = lax.dot_general(
        activation, rows_dy, (((0,), (0,)), ((), ())), preferred_element_type=jnp.float32
    ).astype(jnp.bfloat16)
    in_grad = lax.dot_general(
        rows_x, delta_hidden, (((0,), (0,)), ((), ())), preferred_element_type=jnp.float32
    ).astype(jnp.bfloat16)
    back_rows = lax.dot_general(
        delta_hidden, weight_in, (((1,), (1,)), ((), ())), preferred_element_type=jnp.float32
    ).astype(jnp.bfloat16)
    in_grad, out_grad, back_rows = (
        in_grad[None],
        out_grad[None],
        back_rows.reshape(experts, capacity, quarter),
    )
    returned_back = lax.all_to_all(back_rows, "expert", split_axis=0, concat_axis=0, tiled=True)

    def gather_rows(returned):
        flat_rows = returned.reshape(experts * capacity, quarter)
        return flat_rows[slot_index].astype(jnp.float32).reshape(tok_rows, choose_count, quarter)

    mixed_out = jnp.sum(gather_rows(returned_out) * gate_weights[:, :, None], axis=1).astype(
        jnp.bfloat16
    )
    token_grad = jnp.sum(gather_rows(returned_back), axis=1).astype(jnp.bfloat16)
    return (mixed_out, token_grad, in_grad, out_grad)


BF16, F32 = jnp.bfloat16, jnp.float32
MESH = pl.DeviceIdType.MESH


def mm(a, b, dims=((1,), (0,))):
    return lax.dot_general(a, b, (dims, ((), ())), preferred_element_type=F32)


def fused_kernel(
    n, cap,
    x_ref, dy_ref, ids_ref, gates_ref, win_hbm, wout_hbm,
    mixed_ref, tgrad_ref, ingrad_hbm, outgrad_hbm,
    win_ref, wout_ref, ingrad_ref, outgrad_ref, meta_ref,
    xg, dyg, mg, rows_x, rows_dy, sel, selcat, gate, hp_s, hp_r, sp_s, sp_r, act, delta,
    ocat, osnd, bcat, bsnd, rso_s, rso_r, rsb_s, rsb_r,
    ring_s, ring_r, sib_s, sib_r, mring_s, mring_r, msib_s, msib_r,
    hx_s, hx_r, cx_s, cx_r, rs_s, rs_r, load_sem, ig_sem, og_sem,
):
    half = n // 2
    me = lax.axis_index("expert")
    dp_me = lax.axis_index("dp")
    core = me % 2
    chip = me // 2
    odd = chip % 2
    pos = (chip // 2) * (1 - 2 * odd) + odd * (n - 1)

    def device_at(p):
        hi = p // half
        return ((1 - hi) * 2 * p + hi * (2 * n - 1 - 2 * p)) * 2 + core

    right = {"expert": device_at((pos + 1) % n)}
    left = {"expert": device_at((pos + n - 1) % n)}
    sib = {"expert": me + 1 - 2 * core}
    peer = {"dp": 1 - dp_me}
    ring_to = (right, left)

    load_in = pltpu.make_async_copy(win_hbm, win_ref, load_sem.at[0])
    load_out = pltpu.make_async_copy(wout_hbm, wout_ref, load_sem.at[1])
    load_in.start()
    load_out.start()

    barrier = pltpu.get_barrier_semaphore()
    for d in (right, left, sib, peer):
        pl.semaphore_signal(barrier, inc=1, device_id=d, device_id_type=MESH)
    pl.semaphore_wait(barrier, 4)

    tok = x_ref.shape[0]
    hrow = tok // 2

    def rcopy(src, dst, ssem, rsem, dev):
        return pltpu.make_async_remote_copy(
            src_ref=src, dst_ref=dst, send_sem=ssem, recv_sem=rsem,
            device_id=dev, device_id_type=MESH,
        )

    pending = []
    order = [[0]] + [[(n - h) % n, h] for h in range(1, half)] + [[half]]

    def off(d, h):
        return (-h if d == 0 else h) % n

    def chunks_at(d, h):
        return (0, 1) if h < half else (d,)

    def ring_copy(t, d, h, c):
        own, buf = ((x_ref, xg), (dy_ref, dyg))[t]
        rows = pl.ds(c * hrow, hrow)
        src = own.at[rows] if h == 1 else buf.at[off(d, h - 1), 0, rows]
        return rcopy(src, buf.at[off(d, h), 0, rows], ring_s.at[t, d, h - 1, c], ring_r.at[t, d, h - 1, c], ring_to[d])

    def sib_copy(t, o, c):
        own, buf = ((x_ref, xg), (dy_ref, dyg))[t]
        rows = pl.ds(c * hrow, hrow)
        src = own.at[rows] if o == 0 else buf.at[o, 0, rows]
        return rcopy(src, buf.at[o, 1, rows], sib_s.at[t, o, c], sib_r.at[t, o, c], sib)

    def meta_ring(d, h):
        src = meta_ref if h == 1 else mg.at[off(d, h - 1), 0]
        return rcopy(src, mg.at[off(d, h), 0], mring_s.at[d, h - 1], mring_r.at[d, h - 1], ring_to[d])

    def meta_sib(o):
        src = meta_ref if o == 0 else mg.at[o, 0]
        return rcopy(src, mg.at[o, 1], msib_s.at[o], msib_r.at[o], sib)

    def go(copy):
        copy.start()
        pending.append(copy)

    def send_first(t):
        for c in (0, 1):
            for d in (0, 1):
                go(ring_copy(t, d, 1, c))
        for c in (0, 1):
            go(sib_copy(t, 0, c))

    def send_meta():
        top = ids_ref.shape[0]
        meta_ref[...] = jnp.full(meta_ref.shape, -1.0, F32)
        meta_ref[0:top] = ids_ref[...].astype(F32)
        meta_ref[8:8 + top] = gates_ref[...]
        for d in (0, 1):
            go(meta_ring(d, 1))
        go(meta_sib(0))

    def hop(t, h, between=None):
        if t == 0:
            for d in (0, 1):
                if h < half or d == 0:
                    meta_ring(d, h).wait_recv()
                    if h + 1 < half or (h + 1 == half and d == 0):
                        go(meta_ring(d, h + 1))
                    go(meta_sib(off(d, h)))
        for c in (0, 1):
            if c == 1 and between is not None:
                between()
            for d in (0, 1):
                if c in chunks_at(d, h):
                    ring_copy(t, d, h, c).wait_recv()
                    if h < half and c in chunks_at(d, h + 1):
                        go(ring_copy(t, d, h + 1, c))
                    go(sib_copy(t, off(d, h), c))

    def sib_arrived(t, o):
        for c in (0, 1):
            sib_copy(t, o, c).wait_recv()

    before = (
        lax.broadcasted_iota(jnp.int32, (tok, tok), 0) < lax.broadcasted_iota(jnp.int32, (tok, tok), 1)
    ).astype(F32).astype(BF16)
    slot = lax.broadcasted_iota(jnp.int32, (cap, tok), 0).astype(F32)

    def routing(meta, expert):
        hit = (meta[0:8] == expert).astype(F32)
        g = jnp.sum(hit * meta[8:16], axis=0, keepdims=True)
        named = jnp.sum(hit, axis=0, keepdims=True)
        earlier = mm(jnp.broadcast_to(named, (8, tok)).astype(BF16), before)[0:1]
        chosen = jnp.where(earlier == slot, named, 0.0)
        return chosen.astype(BF16), jnp.sum(chosen * g, axis=1, keepdims=True)

    me_f = me.astype(F32)
    sib_f = (me + 1 - 2 * core).astype(F32)

    def span(o):
        return pl.ds(o * 2 * cap, 2 * cap)

    def take_x(o):
        sib_arrived(0, o)
        meta_sib(o).wait_recv()
        for s in (0, 1):
            first = o == 0 and s == 0
            meta = meta_ref[...] if first else mg[o, s]
            block = x_ref[...] if first else xg[o, s]
            chosen, g = routing(meta, me_f)
            rows = pl.ds(o * 2 * cap + s * cap, cap)
            sel[rows] = chosen
            gate[rows] = g
            rows_x[rows] = mm(chosen, block).astype(BF16)
            if s == 0:
                selcat[pl.ds(o * 2 * cap, cap)] = chosen
                selcat[pl.ds(o * 2 * cap + cap, cap)] = routing(meta, sib_f)[0]
        hp_s[span(o)] = mm(rows_x[span(o)], win_ref[...]).astype(BF16)
        go(dp_copy(0, o))

    def dp_copy(t, o):
        s_buf, r_buf = ((hp_s, hp_r), (sp_s, sp_r))[t]
        return rcopy(s_buf.at[span(o)], r_buf.at[span(o)], hx_s.at[t, o], hx_r.at[t, o], peer)

    def take_dy(o):
        sib_arrived(1, o)
        for s in (0, 1):
            rows = pl.ds(o * 2 * cap + s * cap, cap)
            block = dy_ref[...] if (o == 0 and s == 0) else dyg[o, s]
            rows_dy[rows] = (gate[rows] * mm(sel[rows], block)).astype(BF16)
        sp_s[span(o)] = mm(rows_dy[span(o)], wout_ref[...], ((1,), (1,))).astype(BF16)
        go(dp_copy(1, o))

    def cat_copy(t, o):
        s_buf, r_buf = ((osnd, ocat), (bsnd, bcat))[t]
        return rcopy(
            s_buf.at[pl.ds(o * cap, cap)], r_buf.at[pl.ds(o * 2 * cap + cap, cap)],
            cx_s.at[t, o], cx_r.at[t, o], sib,
        )

    def hidden_of(o):
        return hp_s[span(o)].astype(F32) + hp_r[span(o)].astype(F32)

    def give(t, o, rows):
        s_buf, r_buf = ((osnd, ocat), (bsnd, bcat))[t]
        r_buf[pl.ds(o * 2 * cap, cap)] = rows[:cap]
        s_buf[pl.ds(o * cap, cap)] = rows[cap:]
        go(cat_copy(t, o))

    def forward(o):
        dp_copy(0, o).wait_recv()
        activation = jax.nn.silu(hidden_of(o)).astype(BF16)
        act[span(o)] = activation
        out_rows = mm(activation, wout_ref[...]).astype(BF16)
        give(0, o, (gate[span(o)] * out_rows.astype(F32)).astype(BF16))

    def backward(o):
        dp_copy(1, o).wait_recv()
        slope = sp_s[span(o)].astype(F32) + sp_r[span(o)].astype(F32)
        d_hidden = (slope * silu_slope(hidden_of(o))).astype(BF16)
        delta[span(o)] = d_hidden
        give(1, o, mm(d_hidden, win_ref[...], ((1,), (1,))).astype(BF16))

    def contribution(t, o, c):
        buf = (ocat, bcat)[t]
        return mm(selcat[span(o), c * hrow:(c + 1) * hrow], buf[span(o)], ((0,), (0,)))

    def rs_copy(t, d, h, c):
        s_buf, r_buf = ((rso_s, rso_r), (rsb_s, rsb_r))[t]
        rows = pl.ds(c * hrow, hrow)
        return rcopy(
            s_buf.at[d, h - 1, rows], r_buf.at[d, h - 1, rows],
            rs_s.at[t, d, h - 1, c], rs_r.at[t, d, h - 1, c], ring_to[d],
        )

    def rs_hop(t, h, group):
        s_buf, r_buf = ((rso_s, rso_r), (rsb_s, rsb_r))[t]
        if h == half or group == 0:
            for o in order[h]:
                cat_copy(t, o).wait_recv()
        for d in (0, 1):
            c = d if group else 1 - d
            if c in chunks_at(d, h):
                rows = pl.ds(c * hrow, hrow)
                total = contribution(t, off(1 - d, h), c)
                if h < half and c in chunks_at(d, h + 1):
                    rs_copy(t, d, h + 1, c).wait_recv()
                    total = total + r_buf[d, h, rows].astype(F32)
                s_buf[d, h - 1, rows] = total.astype(BF16)
                go(rs_copy(t, d, h, c))

    def rs_last(t):
        r_buf = (rso_r, rsb_r)[t]
        out = (mixed_ref, tgrad_ref)[t]
        cat_copy(t, 0).wait_recv()
        for c in (0, 1):
            rows = pl.ds(c * hrow, hrow)
            total = contribution(t, 0, c)
            for d in (0, 1):
                rs_copy(t, d, 1, c).wait_recv()
                total = total + r_buf[d, 0, rows].astype(F32)
            out[rows] = total.astype(BF16)

    def grad_tile(i, left, right, v_ref, hbm, sem):
        cols = slice(i * tile, (i + 1) * tile)
        v_ref[cols] = mm(left[:, cols], right[...], ((0,), (0,))).astype(BF16)
        copy = pltpu.make_async_copy(v_ref.at[cols], hbm.at[cols], sem.at[i])
        copy.start()
        stores.append(copy)

    def out_tiles(tiles):
        for i in tiles:
            grad_tile(i, act, rows_dy, outgrad_ref, outgrad_hbm, og_sem)

    def in_tiles(tiles):
        for i in tiles:
            grad_tile(i, rows_x, delta, ingrad_ref, ingrad_hbm, ig_sem)

    stores = []
    tile = 256
    n_out, n_in = act.shape[1] // tile, rows_x.shape[1] // tile

    def each(f, i):
        for o in order[i]:
            f(o)

    send_first(0)
    send_meta()
    load_in.wait()
    take_x(0)
    for h in range(1, half):
        hop(0, h)
        if h == half - 1:
            send_first(1)
            load_out.wait()
        each(take_x, h)
    hop(0, half)
    take_x(half)
    for h in range(1, half - 1):
        hop(1, h, lambda: each(take_dy, h - 1))
        each(forward, h - 1)
    hop(1, half - 1, lambda: each(forward, half))
    rs_hop(0, half, 1)
    each(take_dy, half - 2)
    each(forward, half - 1)
    rs_hop(0, half - 1, 0)
    hop(1, half)
    each(take_dy, half - 1)
    rs_hop(0, half - 1, 1)
    each(forward, half - 2)
    fill = [lambda: each(take_dy, half)]
    for i in range(half - 1):
        fill += [functools.partial(backward, o) for o in order[i]]
    fill += [functools.partial(out_tiles, [i]) for i in range(n_out - 1)]
    steps = [(h, g) for h in range(half - 2, 0, -1) for g in (0, 1)]

    def spread(t, steps, fill):
        for i, (h, g) in enumerate(steps):
            rs_hop(t, h, g)
            for f in fill[len(fill) * i // len(steps):len(fill) * (i + 1) // len(steps)]:
                f()

    spread(0, steps, fill)
    each(backward, half)
    rs_hop(1, half, 1)
    each(backward, half - 1)
    rs_hop(1, half - 1, 0)
    rs_last(0)
    fill = [functools.partial(in_tiles, [i]) for i in range(n_in)]
    fill += [functools.partial(out_tiles, [n_out - 1])]
    spread(1, [(half - 1, 1)] + steps, fill)
    rs_last(1)
    for copy in stores:
        copy.wait()
    for copy in pending:
        copy.wait_send()


def copy_kernel(count, *refs):
    srcs, dsts, bufs = refs[:count], refs[count:2 * count], refs[2 * count:3 * count]
    in_sem, out_sem = refs[3 * count:]
    into, outof = [], []
    for j in range(count):
        rows = srcs[j].shape[0] // 4
        for q in range(4):
            at = pl.ds(q * rows, rows)
            into.append(pltpu.make_async_copy(srcs[j].at[at], bufs[j].at[at], in_sem.at[j, q]))
            outof.append(pltpu.make_async_copy(bufs[j].at[at], dsts[j].at[at], out_sem.at[j, q]))
    for copy in into:
        copy.start()
    for a, b in zip(into, outof):
        a.wait()
        b.start()
    for copy in outof:
        copy.wait()


def settle(arrays):
    count = len(arrays)
    return pl.pallas_call(
        functools.partial(copy_kernel, count),
        out_shape=[jax.ShapeDtypeStruct(a.shape, a.dtype) for a in arrays],
        in_specs=[pl.BlockSpec(memory_space=pl.ANY)] * count,
        out_specs=[pl.BlockSpec(memory_space=pl.ANY)] * count,
        scratch_shapes=[pltpu.VMEM(a.shape, a.dtype) for a in arrays]
        + [pltpu.SemaphoreType.DMA((count, 4))] * 2,
        name="settle",
    )(*arrays)


def local_fused(tokens, cotangent, expert_ids, gate_weights, w_in, w_out):
    experts = lax.axis_size("expert")
    tok_rows, width = tokens.shape
    top = expert_ids.shape[1]
    hid = w_in.shape[2]
    cap = max(2, 4 * tok_rows * top // (3 * experts))
    n = experts // 2
    half = n // 2
    slots = experts * cap
    vm = pltpu.VMEM
    dma = pltpu.SemaphoreType.DMA
    mixed, tgrad, ingrad, outgrad = pl.pallas_call(
        functools.partial(fused_kernel, n, cap),
        out_shape=(
            jax.ShapeDtypeStruct((tok_rows, width), BF16),
            jax.ShapeDtypeStruct((tok_rows, width), BF16),
            jax.ShapeDtypeStruct((width, hid), BF16),
            jax.ShapeDtypeStruct((hid, width), BF16),
        ),
        in_specs=[pl.BlockSpec(memory_space=pltpu.VMEM)] * 4 + [pl.BlockSpec(memory_space=pl.ANY)] * 2,
        out_specs=[pl.BlockSpec(memory_space=pltpu.VMEM)] * 2 + [pl.BlockSpec(memory_space=pl.ANY)] * 2,
        scratch_shapes=[
            vm((width, hid), BF16),
            vm((hid, width), BF16),
            vm((width, hid), BF16),
            vm((hid, width), BF16),
            vm((16, tok_rows), F32),
            vm((n, 2, tok_rows, width), BF16),
            vm((n, 2, tok_rows, width), BF16),
            vm((n, 2, 16, tok_rows), F32),
            vm((slots, width), BF16),
            vm((slots, width), BF16),
            vm((slots, tok_rows), BF16),
            vm((slots, tok_rows), BF16),
            vm((slots, 1), F32),
            vm((slots, hid), BF16),
            vm((slots, hid), BF16),
            vm((slots, hid), BF16),
            vm((slots, hid), BF16),
            vm((slots, hid), BF16),
            vm((slots, hid), BF16),
            vm((slots, width), BF16),
            vm((slots // 2, width), BF16),
            vm((slots, width), BF16),
            vm((slots // 2, width), BF16),
            vm((2, half, tok_rows, width), BF16),
            vm((2, half, tok_rows, width), BF16),
            vm((2, half, tok_rows, width), BF16),
            vm((2, half, tok_rows, width), BF16),
            dma((2, 2, half, 2)),
            dma((2, 2, half, 2)),
            dma((2, n, 2)),
            dma((2, n, 2)),
            dma((2, half)),
            dma((2, half)),
            dma((n,)),
            dma((n,)),
            dma((2, n)),
            dma((2, n)),
            dma((2, n)),
            dma((2, n)),
            dma((2, 2, half, 2)),
            dma((2, 2, half, 2)),
            dma((2,)),
            dma((width // 256,)),
            dma((hid // 256,)),
        ],
        compiler_params=pltpu.CompilerParams(
            collective_id=0, has_side_effects=True, vmem_limit_bytes=67043328
        ),
        name="fused_experts",
    )(tokens, cotangent, expert_ids.T, gate_weights.T, w_in[0], w_out[0])
    mixed, tgrad, ingrad, outgrad = settle([mixed, tgrad, ingrad, outgrad])
    return (mixed, tgrad, ingrad[None], outgrad[None])


def gathers_pay(mesh, tok_rows, top, width, hid):
    experts = mesh.shape["expert"]
    cap = max(2, 4 * tok_rows * top // (3 * experts))
    return (
        mesh.shape["dp"] == 2
        and experts % 8 == 0
        and top <= 8
        and tok_rows % 128 == 0
        and cap % 16 == 0
        and tok_rows <= 2 * cap
        and width % 256 == 0
        and hid % 256 == 0
    )


def solution(mesh):
    in_specs = (
        P("expert", "dp"),
        P("expert", "dp"),
        P("expert", None),
        P("expert", None),
        P("expert", "dp", None),
        P("expert", None, "dp"),
    )
    out_specs = (
        P("expert", "dp"),
        P("expert", "dp"),
        P("expert", "dp", None),
        P("expert", None, "dp"),
    )

    def run(tokens, cotangent, expert_ids, gate_weights, w_in, w_out):
        rows, top = expert_ids.shape
        width = tokens.shape[1] // mesh.shape["dp"]
        fused = gathers_pay(mesh, rows // mesh.shape["expert"], top, width, w_in.shape[2])
        body = jax.shard_map(
            local_fused if fused else local_slots,
            mesh=mesh, in_specs=in_specs, out_specs=out_specs, check_vma=False,
        )
        return body(tokens, cotangent, expert_ids, gate_weights, w_in, w_out)

    return run
```
